32 devices in a mesh: groups: 2 (over y), tm: 4 (over z), space: 2 (over x), mp: 2 (over core).
Axes of the slice: x: 2, y: 2, z: 4, core: 2. Of those that a mesh axis runs over, the one named last changes fastest.
Arguments:
- query_proj: bfloat16 [16, 16, 8, 2240], P(('groups', 'tm'), 'space', None, 'mp'), parts along dimension 0, may hold values from -6 to 6
- key_proj: bfloat16 [16, 16, 8, 2240], P(('groups', 'tm'), 'space', None, 'mp'), parts along dimension 0, may hold values from -6 to 6
- value_proj: bfloat16 [16, 16, 8, 2240], P(('groups', 'tm'), 'space', None, 'mp'), parts along dimension 0, may hold values from -6 to 6
- expanded: bfloat16 [16, 16, 8, 2, 6720], P(('groups', 'tm'), 'space', None, None, 'mp'), parts along dimension 0, may hold values from -6 to 6
- spatial_weight: float32 [3, 3, 2, 6720], P(None, None, None, 'mp'), may hold values from -0.6 to 0.6
- temporal_weight: float32 [3, 2, 6720], P(None, None, 'mp'), may hold values from -1 to 1
Outputs:
- attended: bfloat16 [16, 16, 8, 2240], P(('groups', 'tm'), 'space', None, 'mp'), parts along dimension 0
- gated_hidden: bfloat16 [16, 16, 8, 6720], P(('groups', 'tm'), 'space', None, 'mp'), parts along dimension 0
The draws below stay inside these ranges and needn't reach their ends.
There are 2 independent parts, one for each index of `groups`. The reference program is written for one: setup_inputs(seed, part) draws one part's arguments, and reference() takes and returns one part's arrays. A program takes and returns all parts, laid end to end along the dimension named above; an argument that names none is the same for every part. Nothing has to cross between parts.
All inputs are finite; a program needn't handle non-finite values.
Results may differ from the reference program's by a relative error of at most 0.0059.
Values may be sent and summed in bfloat16 or wider, within the bound.
No kernel may reach another device: no remote copies, remote signals or barrier semaphores. Data moves between devices by JAX's collectives and lax.ppermute only.
A program may use at most 64 MiB of HBM per device.

```python
import jax
import jax.numpy as jnp
from jax import lax

HEADS = 70
HEAD_DIM = 32
FF = 6720
FR_DEV = 2
WIDTH_CELLS = 8
CH = 2240
FRAMES = 8
HEIGHT = 16
N_TM = 4


def block_scale(rng, dims, shards, low, high):
    def one(axis_at, shards_of):
        draws = jax.random.uniform(jax.random.fold_in(jax.random.fold_in(rng, 6), axis_at), (shards_of,), jnp.float32, low / len(shards), high / len(shards))
        return jnp.repeat(jnp.exp(draws), dims[axis_at] // shards_of).reshape((-1,) + (1,) * (len(dims) - axis_at - 1))

    factor_of = one(*shards[0])
    for cut in shards[1:]:
        factor_of = factor_of * one(*cut)
    return factor_of


def gaussian(own_key, shape, scale, reach, pieces=(), kind=jnp.bfloat16):
    array = jax.random.normal(own_key, shape, jnp.float32) * scale
    if len(pieces) > 0:
        array = block_scale(own_key, shape, pieces, -0.22, 0.18) * array
    return jnp.clip(array, min=-reach, max=reach).astype(kind)


def setup_inputs(seed: int = 0, part: int = 0) -> dict:
    key_of = jax.random.split(jax.random.key(seed), 7)
    part_keys = jax.random.split(jax.random.fold_in(key_of[6], part), 7)
    return {
        "query_proj": gaussian(part_keys[0], (FRAMES, HEIGHT, WIDTH_CELLS, CH), 1.0, 6.0, ((0, 4), (1, 2), (3, 2))),
        "key_proj": gaussian(part_keys[1], (FRAMES, HEIGHT, WIDTH_CELLS, CH), 1.0, 6.0, ((0, 4), (1, 2), (3, 2))),
        "value_proj": gaussian(part_keys[2], (FRAMES, HEIGHT, WIDTH_CELLS, CH), 1.0, 6.0, ((0, 4), (1, 2), (3, 2))),
        "expanded": gaussian(part_keys[3], (FRAMES, HEIGHT, WIDTH_CELLS, 2, FF), 1.0, 6.0, ((0, 4), (1, 2), (4, 2))),
        "spatial_weight": jnp.clip(jax.random.uniform(key_of[4], (3, 3, 2, FF), jnp.float32, -0.6, 0.6) * block_scale(key_of[4], (3, 3, 2, FF), ((3, 2),), -0.4, 0.0), -0.6, 0.6),
        "temporal_weight": jnp.clip(jax.random.uniform(key_of[5], (3, 2, FF), jnp.float32, -1.0, 1.0) * block_scale(key_of[5], (3, 2, FF), ((2, 2),), -0.4, 0.0), -1.0, 1.0),
    }


def conv_plane(plane, spatial_weight):
    row_count = plane.shape[0]
    col_count = plane.shape[1]
    padded = jnp.pad(plane, ((1, 1), (1, 1), (0, 0), (0, 0)))
    summed = jnp.zeros(plane.shape, jnp.float32)
    for row_tap in range(3):
        for col_tap in range(3):
            summed = summed + padded[row_tap:row_tap + row_count, col_tap:col_tap + col_count].astype(jnp.float32) * spatial_weight[row_tap, col_tap]
    return summed.astype(jnp.bfloat16)


def reference(query_proj, key_proj, value_proj, expanded, spatial_weight, temporal_weight):
    tokens_frame = HEIGHT * WIDTH_CELLS
    key_relu = jnp.maximum(key_proj, 0).reshape(FRAMES, tokens_frame, HEADS, HEAD_DIM).astype(jnp.float32)
    value_all = value_proj.reshape(FRAMES, tokens_frame, HEADS, HEAD_DIM).astype(jnp.float32)
    frame_state = jnp.einsum('fthd,fthe->fdhe', key_relu, value_all, precision=lax.Precision.HIGHEST)
    frame_keys = jnp.sum(key_relu, axis=1)
    span_state = frame_state.reshape(N_TM, FR_DEV, HEAD_DIM, HEADS, HEAD_DIM).sum(axis=1)
    span_keys = frame_keys.reshape(N_TM, FR_DEV, HEADS, HEAD_DIM).sum(axis=1)
    state_prefix = jnp.cumsum(span_state, axis=0)
    keys_prefix = jnp.cumsum(span_keys, axis=0)
    query_relu = jnp.maximum(query_proj, 0).reshape(N_TM, FR_DEV * tokens_frame, HEADS, HEAD_DIM).astype(jnp.float32)
    numerator = jnp.einsum('cthd,cdhe->cthe', query_relu, state_prefix, precision=lax.Precision.HIGHEST)
    denominator = jnp.einsum('cthd,chd->cth', query_relu, keys_prefix, precision=lax.Precision.HIGHEST) + 1.0
    attended = (numerator / denominator[..., None]).reshape(FRAMES, HEIGHT, WIDTH_CELLS, CH).astype(jnp.bfloat16)

    def spatial_frame(plane):
        return conv_plane(plane, spatial_weight)

    spatial = lax.map(spatial_frame, expanded)
    padded_time = jnp.concatenate([jnp.zeros((2,) + spatial.shape[1:], jnp.bfloat16), spatial], axis=0)

    def temporal_frame(frame_index):
        window = lax.dynamic_slice_in_dim(padded_time, frame_index, 3, 0).astype(jnp.float32)
        mixed = window[0] * temporal_weight[0] + window[1] * temporal_weight[1] + window[2] * temporal_weight[2]
        return (mixed[..., 0, :] * jax.nn.silu(mixed[..., 1, :])).astype(jnp.bfloat16)

    gated_hidden = lax.map(temporal_frame, jnp.arange(FRAMES, dtype=jnp.int32))
    return attended, gated_hidden
```

```python
import functools

import jax
import jax.numpy as jnp
from jax import lax
from jax.experimental import pallas as pl
from jax.experimental.pallas import tpu as pltpu
from jax.sharding import PartitionSpec as P

HEAD_DIM = 32
LANES = 128
STATE_ROWS = HEAD_DIM + 8
F32 = jnp.float32
BF16 = jnp.bfloat16


def shifted(value, axis, steps):
    count = lax.axis_size(axis)
    first, last = (max(0, -steps), min(count, count - steps))
    return lax.ppermute(value, axis, [(source, source + steps) for source in range(first, last)])


def rotated(value, axis, steps):
    count = lax.axis_size(axis)
    return lax.ppermute(value, axis, [(source, (source + steps) % count) for source in range(count)])


def edge_rows(frame):
    count, mine = (lax.axis_size("space"), lax.axis_index("space"))
    head, tail = (frame[:, 0], frame[:, -1])
    if count == 2:
        other = lax.ppermute(jnp.where(mine == 0, tail, head), "space", [(0, 1), (1, 0)])
        return (other, other)
    return (shifted(tail, "space", 1), shifted(head, "space", -1))


def params(vmem_mib=16):
    return pltpu.CompilerParams(vmem_limit_bytes=vmem_mib << 20)


VMEM = pl.BlockSpec(memory_space=pltpu.VMEM)
SMEM = pl.BlockSpec(memory_space=pltpu.SMEM)


def lane_tiles(channels, body):
    full = channels // LANES

    @pl.loop(0, full)
    def _(tile):
        body(pl.ds(pl.multiple_of(tile * LANES, LANES), LANES), LANES)

    if channels % LANES:
        body(pl.ds(full * LANES, channels % LANES), channels % LANES)


def tap_weights(weight_ref, part, lanes, width, columns):
    column = lax.broadcasted_iota(jnp.int32, (columns, width), 0)
    taps = []
    for row_tap in range(3):
        row = []
        for col_tap in range(3):
            w = jnp.broadcast_to(weight_ref[row_tap, col_tap, part : part + 1, lanes], (columns, width))
            if col_tap == 0:
                w = jnp.where(column == columns - 1, 0.0, w)
            if col_tap == 2:
                w = jnp.where(column == 0, 0.0, w)
            row.append(w)
        taps.append(row)
    return taps


def conv_rows(rows, taps, columns):
    out = []
    for r in range(len(rows) - 2):
        column_sums = [
            taps[0][b] * rows[r] + taps[1][b] * rows[r + 1] + taps[2][b] * rows[r + 2] for b in range(3)
        ]
        total = (
            column_sums[1]
            + pltpu.roll(column_sums[0], 1, 0)
            + pltpu.roll(column_sums[2], columns - 1, 0)
        )
        out.append(total.astype(BF16))
    return out


def padded_rows(frame_ref, top, bottom, part, lanes):
    row_count = frame_ref.shape[1]
    return (
        [top]
        + [frame_ref[part, r, :, lanes].astype(F32) for r in range(row_count)]
        + [bottom]
    )


def masked(edge_ref, part, lanes, flag):
    return edge_ref[part, :, lanes].astype(F32) * flag


def own_conv_kernel(flags, f0, f1, top0, top1, bot0, bot1, weight, s0, s1):
    columns = f0.shape[2]
    has_top, has_bottom = (flags[0].astype(F32), flags[1].astype(F32))

    def tile(lanes, width):
        for part in range(2):
            taps = tap_weights(weight, part, lanes, width, columns)
            for frame, top, bottom, out in ((f0, top0, bot0, s0), (f1, top1, bot1, s1)):
                rows = padded_rows(
                    frame,
                    masked(top, part, lanes, has_top),
                    masked(bottom, part, lanes, has_bottom),
                    part,
                    lanes,
                )
                for r, value in enumerate(conv_rows(rows, taps, columns)):
                    out[part, r, :, lanes] = value

    lane_tiles(f0.shape[3], tile)


def gate(value, key):
    return value * (key / (1.0 + jnp.exp(-key)))


def mix_kernel(taps_of, flags, raw, top, bottom, near0, near1, weight, temporal, out):
    columns = raw.shape[2]
    has_top, has_bottom = (flags[0].astype(F32), flags[1].astype(F32))

    def tile(lanes, width):
        mixed = []
        for part in range(2):
            taps = tap_weights(weight, part, lanes, width, columns)
            rows = padded_rows(
                raw,
                masked(top, part, lanes, has_top),
                masked(bottom, part, lanes, has_bottom),
                part,
                lanes,
            )
            w = [
                jnp.broadcast_to(temporal[tap, part : part + 1, lanes], (columns, width)) for tap in taps_of
            ]
            mixed.append(
                [
                    w[0] * value.astype(F32)
                    + w[1] * near0[part, r, :, lanes].astype(F32)
                    + w[2] * near1[part, r, :, lanes].astype(F32)
                    for r, value in enumerate(conv_rows(rows, taps, columns))
                ]
            )
        for r in range(raw.shape[1]):
            out[r, :, lanes] = gate(mixed[0][r], mixed[1][r]).astype(BF16)

    lane_tiles(raw.shape[3], tile)


def first_kernel(s0, temporal, out):
    columns = s0.shape[2]

    def tile(lanes, width):
        w = [jnp.broadcast_to(temporal[2, part : part + 1, lanes], (columns, width)) for part in range(2)]
        for r in range(s0.shape[1]):
            mixed = [w[part] * s0[part, r, :, lanes].astype(F32) for part in range(2)]
            out[r, :, lanes] = gate(mixed[0], mixed[1]).astype(BF16)

    lane_tiles(s0.shape[3], tile)


def own_conv(flags, f0, f1, edges0, edges1, weight):
    return pl.pallas_call(
        own_conv_kernel,
        out_shape=(jax.ShapeDtypeStruct(f0.shape, BF16),) * 2,
        in_specs=[SMEM] + [VMEM] * 7,
        out_specs=(VMEM, VMEM),
        compiler_params=params(),
        name="own_conv",
    )(flags, f0, f1, edges0[0], edges1[0], edges0[1], edges1[1], weight)


def mix(taps_of, flags, raw, edges, near0, near1, weight, temporal, name):
    return pl.pallas_call(
        functools.partial(mix_kernel, taps_of),
        out_shape=jax.ShapeDtypeStruct(raw.shape[1:], BF16),
        in_specs=[SMEM] + [VMEM] * 7,
        out_specs=VMEM,
        compiler_params=params(),
        name=name,
    )(flags, raw, edges[0], edges[1], near0, near1, weight, temporal)


def first_frame(s0, temporal):
    return pl.pallas_call(
        first_kernel,
        out_shape=jax.ShapeDtypeStruct(s0.shape[1:], BF16),
        in_specs=[VMEM] * 2,
        out_specs=VMEM,
        compiler_params=params(),
        name="first_frame",
    )(s0, temporal)


def head_mask(width):
    row = lax.broadcasted_iota(jnp.int32, (width, width), 0) // HEAD_DIM
    column = lax.broadcasted_iota(jnp.int32, (width, width), 1) // HEAD_DIM
    return row == column


def lane_groups(channels):
    return [(at, min(LANES, channels - at)) for at in range(0, channels, LANES)]


def state_kernel(key, value, state):
    tokens, channels = key.shape
    chunk = state.shape[2]
    ones = jnp.ones((8, tokens), BF16)
    state[...] = jnp.zeros_like(state)
    for at, width in lane_groups(channels):
        keys = jnp.maximum(key[:, at : at + width], 0)
        product = lax.dot_general(
            keys, value[:, at : at + width], (((0,), (0,)), ((), ())), preferred_element_type=F32
        )
        product = jnp.where(head_mask(width), product, 0.0)
        folded = sum(product[d : d + HEAD_DIM] for d in range(0, width, HEAD_DIM))
        lanes = slice(at % chunk, at % chunk + width)
        state[at // chunk, :HEAD_DIM, lanes] = folded
        state[at // chunk, HEAD_DIM:, lanes] = jnp.dot(ones, keys, preferred_element_type=F32)


def split(value):
    high = value.astype(BF16)
    return (high, (value - high.astype(F32)).astype(BF16))


def attend_kernel(query, state, out):
    channels = query.shape[1]
    chunk = state.shape[2]
    for at, width in lane_groups(channels):
        rows = jnp.maximum(query[:, at : at + width], 0)
        lanes = slice(at % chunk, at % chunk + width)
        mask = head_mask(width)
        folded = state[at // chunk, :HEAD_DIM, lanes]
        kv = jnp.where(mask, jnp.concatenate([folded] * (width // HEAD_DIM), axis=0), 0.0)
        sums = jnp.where(
            mask, jnp.broadcast_to(state[at // chunk, HEAD_DIM : HEAD_DIM + 1, lanes], (width, width)), 0.0
        )
        numerator = sum(jnp.dot(rows, part, preferred_element_type=F32) for part in split(kv))
        denominator = sum(
            lax.dot_general(rows, part, (((1,), (1,)), ((), ())), preferred_element_type=F32)
            for part in split(sums)
        )
        out[:, at : at + width] = (numerator / (denominator + 1.0)).astype(BF16)


def local_state(key, value, chunks):
    channels = key.shape[1]
    groups = pl.cdiv(pl.cdiv(channels, LANES), chunks)
    return pl.pallas_call(
        state_kernel,
        out_shape=jax.ShapeDtypeStruct((chunks, STATE_ROWS, groups * LANES), F32),
        in_specs=[VMEM] * 2,
        out_specs=VMEM,
        compiler_params=params(),
        name="local_state",
    )(key, value)


def attend(query, state):
    return pl.pallas_call(
        attend_kernel,
        out_shape=jax.ShapeDtypeStruct(query.shape, BF16),
        in_specs=[VMEM] * 2,
        out_specs=VMEM,
        compiler_params=params(),
        name="attend",
    )(query, state)


def prefixed_state(state):
    count, mine = (lax.axis_size("space"), lax.axis_index("space"))
    own = lax.dynamic_index_in_dim(state, mine, 0, keepdims=False)
    for step in range(1, count):
        chunk = lax.dynamic_index_in_dim(state, (mine + step) % count, 0, keepdims=False)
        own = own + rotated(chunk, "space", step)
    step = 1
    while step < lax.axis_size("tm"):
        own = own + shifted(own.astype(BF16), "tm", step).astype(F32)
        step *= 2
    whole = lax.dynamic_update_index_in_dim(state, own, mine, 0)
    for step in range(1, count):
        whole = lax.dynamic_update_index_in_dim(
            whole, rotated(own, "space", step), (mine - step) % count, 0
        )
    return whole


def on_device(query_proj, key_proj, value_proj, expanded, spatial_weight, temporal_weight):
    frames, row_count, col_count, channels = query_proj.shape
    assert frames == 2
    space, spaces = (lax.axis_index("space"), lax.axis_size("space"))
    flags = jnp.stack([space > 0, space < spaces - 1]).astype(jnp.int32)

    f0, f1 = (jnp.transpose(expanded[t], (2, 0, 1, 3)) for t in range(2))
    before = shifted(f1, "tm", 1)
    after = shifted(f0, "tm", -1)
    both = edge_rows(jnp.concatenate([f0, f1], axis=0))
    edges0, edges1 = ([edge[2 * t : 2 * t + 2] for edge in both] for t in range(2))

    def tokens(array):
        return array.reshape(-1, channels)

    state = local_state(tokens(key_proj), tokens(value_proj), spaces)
    whole = prefixed_state(state)
    attended = attend(tokens(query_proj), whole).reshape(query_proj.shape)

    s0, s1 = own_conv(flags, f0, f1, edges0, edges1, spatial_weight)
    theirs = mix(
        (2, 0, 1), flags, after, edge_rows(after), s0, s1, spatial_weight, temporal_weight, "mix_after"
    )
    out1 = mix(
        (0, 1, 2), flags, before, edge_rows(before), s0, s1, spatial_weight, temporal_weight, "mix_before"
    )
    out0 = shifted(theirs, "tm", 1)
    out0 = jnp.where(lax.axis_index("tm") == 0, first_frame(s0, temporal_weight), out0)
    return (attended, jnp.stack([out0, out1]))


def solution(mesh):
    return jax.shard_map(
        on_device,
        mesh=mesh,
        in_specs=(
            P(("groups", "tm"), "space", None, "mp"),
            P(("groups", "tm"), "space", None, "mp"),
            P(("groups", "tm"), "space", None, "mp"),
            P(("groups", "tm"), "space", None, None, "mp"),
            P(None, None, None, "mp"),
            P(None, None, "mp"),
        ),
        out_specs=(
            P(("groups", "tm"), "space", None, "mp"),
            P(("groups", "tm"), "space", None, "mp"),
        ),
        check_vma=False,
    )
```

```python
import functools

import jax
import jax.numpy as jnp
from jax import lax
from jax.experimental import pallas as pl
from jax.experimental.pallas import tpu as pltpu
from jax.sharding import PartitionSpec as P

HEAD_DIM = 32
LANES = 128
STATE_ROWS = HEAD_DIM + 8
BLOCK = 8
SENT_ROWS = 5
F32 = jnp.float32
BF16 = jnp.bfloat16


def permuted(value, axis, pairs):
    return lax.ppermute(value, axis, pairs)


def shifted(value, axis, steps):
    count = lax.axis_size(axis)
    first, last = (max(0, -steps), min(count, count - steps))
    return permuted(value, axis, [(source, source + steps) for source in range(first, last)])


def rotated(value, axis, steps):
    count = lax.axis_size(axis)
    return permuted(value, axis, [(source, (source + steps) % count) for source in range(count)])


VMEM = pl.BlockSpec(memory_space=pltpu.VMEM)
SMEM = pl.BlockSpec(memory_space=pltpu.SMEM)
ANY = pl.BlockSpec(memory_space=pl.ANY)


def kernel_call(kernel, out_shape, operands, specs=None, out_specs=None, scratch=(), aliases=None, vmem_mib=16):
    many = isinstance(out_shape, tuple)
    return pl.pallas_call(
        kernel,
        out_shape=out_shape,
        in_specs=[VMEM] * len(operands) if specs is None else specs,
        out_specs=out_specs if out_specs is not None else ((VMEM,) * len(out_shape) if many else VMEM),
        scratch_shapes=scratch,
        input_output_aliases=aliases or {},
        compiler_params=pltpu.CompilerParams(vmem_limit_bytes=vmem_mib << 20),
    )(*operands)


def lane_tiles(channels, body):
    full = channels // LANES

    @pl.loop(0, full)
    def _(tile):
        body(pl.ds(pl.multiple_of(tile * LANES, LANES), LANES), LANES)

    if channels % LANES:
        body(pl.ds(full * LANES, channels % LANES), channels % LANES)


def spread(row, columns, width):
    return jnp.broadcast_to(row, (columns, width))


def tap_weights(weight_ref, part, lanes, width, columns):
    column = lax.broadcasted_iota(jnp.int32, (columns, width), 0)
    taps = []
    for row_tap in range(3):
        row = []
        for col_tap in range(3):
            w = spread(weight_ref[row_tap, col_tap, part : part + 1, lanes], columns, width)
            if col_tap == 0:
                w = jnp.where(column == columns - 1, 0.0, w)
            if col_tap == 2:
                w = jnp.where(column == 0, 0.0, w)
            row.append(w)
        taps.append(row)
    return taps


def conv_row(above, here, below, taps, columns):
    sums = [taps[0][b] * above + taps[1][b] * here + taps[2][b] * below for b in range(3)]
    total = sums[1] + pltpu.roll(sums[0], 1, 0) + pltpu.roll(sums[2], columns - 1, 0)
    return total.astype(BF16)


def conv_interior(load, wanted, taps, columns):
    held = {}

    def row(r):
        if r not in held:
            held[r] = load(r)
        return held[r]

    return [conv_row(row(r - 1), row(r), row(r + 1), taps, columns) for r in wanted]


def interior_kernel(jobs, frames, weight, out):
    columns, channels = frames.shape[3:]

    def tile(lanes, width):
        for part in range(2):
            taps = tap_weights(weight, part, lanes, width, columns)
            at = 0
            for frame, wanted in jobs:

                def load(r, frame=frame, part=part):
                    return frames[frame, r, part, :, lanes].astype(F32)

                for value in conv_interior(load, wanted, taps, columns):
                    out[at, part, :, lanes] = value
                    at += 1

    lane_tiles(channels, tile)


def interior(frames, weight, jobs):
    rows = sum(len(wanted) for _, wanted in jobs)
    return kernel_call(
        functools.partial(interior_kernel, jobs),
        jax.ShapeDtypeStruct((rows,) + frames.shape[2:], BF16),
        (frames, weight),
    )


def slab_places(chunk, channels):
    per_slab = channels // chunk
    return [(block // per_slab, block % per_slab * chunk) for block in range(STATE_ROWS // BLOCK)]


def pack_kernel(edges, index, frames, state, out):
    row_count, _, columns, channels = frames.shape[1:]
    chunk = state.shape[2]
    at = 0
    if edges is not None:
        for frame in range(2):
            for part in range(2):
                if edges == "either":
                    first = index[1] == 0

                    @pl.when(first)
                    def _(frame=frame, part=part, at=at):
                        out[at] = frames[frame, row_count - 1, part]

                    @pl.when(jnp.logical_not(first))
                    def _(frame=frame, part=part, at=at):
                        out[at] = frames[frame, 0, part]

                else:
                    out[at] = frames[frame, 0 if edges == "head" else row_count - 1, part]
                at += 1
    places = slab_places(chunk, channels)
    for slab in range(places[-1][0] + 1):
        out[at + slab] = jnp.zeros((columns, channels), BF16)
    for block, (slab, lane) in enumerate(places):
        out[at + slab, :, lane : lane + chunk] = state[
            index[0], block * BLOCK : (block + 1) * BLOCK, :
        ].astype(BF16)


def boundary_kernel(n_packs, first_of, top_at, bottom_at, info, frames, weight, state, *refs):
    packs, (out, total) = (refs[:n_packs], refs[n_packs:])
    row_count, _, columns, channels = frames.shape[1:]
    has_top, has_bottom = (info[0].astype(F32), info[1].astype(F32))
    chunk = state.shape[2]

    def tile(lanes, width):
        for part in range(2):
            taps = tap_weights(weight, part, lanes, width, columns)
            for frame in range(2):

                def load(r, frame=frame, part=part):
                    if r < 0:
                        return packs[top_at][2 * frame + part, :, lanes].astype(F32) * has_top
                    if r == row_count:
                        return packs[bottom_at][2 * frame + part, :, lanes].astype(F32) * has_bottom
                    return frames[frame, r, part, :, lanes].astype(F32)

                for i, value in enumerate(conv_interior(load, (0, row_count - 1), taps, columns)):
                    out[2 * frame + i, part, :, lanes] = value

    lane_tiles(channels, tile)
    for block, (slab, lane) in enumerate(slab_places(chunk, channels)):
        rows = slice(block * BLOCK, (block + 1) * BLOCK)
        value = state[info[2], rows, :]
        for pack, first in zip(packs, first_of):
            value = value + pack[first + slab, :, lane : lane + chunk].astype(F32)
        total[rows, :] = value


def gate(value, key):
    return value * (key / (1.0 + jnp.exp(-key)))


def theirs_kernel(raw, s0, s1, weight, temporal, out):
    columns, channels = raw.shape[2:]
    count = out.shape[0]

    def tile(lanes, width):
        mixed = []
        for part in range(2):
            taps = tap_weights(weight, part, lanes, width, columns)
            w = [spread(temporal[tap, part : part + 1, lanes], columns, width) for tap in range(3)]

            def load(r, part=part):
                return raw[r, part, :, lanes].astype(F32)

            mixed.append(
                [
                    w[0] * s0[r, part, :, lanes].astype(F32)
                    + w[1] * s1[r, part, :, lanes].astype(F32)
                    + w[2] * value.astype(F32)
                    for r, value in enumerate(conv_interior(load, range(1, count + 1), taps, columns))
                ]
            )
        for r in range(count):
            out[r, :, lanes] = gate(mixed[0][r], mixed[1][r]).astype(BF16)

    lane_tiles(channels, tile)


def ours_kernel(sent, info, mine_a, mine_b, mine_s0, before_a, before_b, temporal, out, frame0, frame1, sems):
    row_count, columns, channels = frame1.shape
    inner = row_count - 2

    def spatial(a, b, frame, r, part, lanes):
        if r in (0, row_count - 1):
            ref, at = (b, 2 * frame + (r > 0))
        elif frame == 1:
            ref, at = (a, r - 1)
        elif r > sent:
            ref, at = (a, inner + r - sent - 1)
        else:
            ref, at = (mine_s0, r - 1)
        return ref[at, part, :, lanes].astype(F32)

    def weights(lanes, width):
        return [
            [spread(temporal[tap, part : part + 1, lanes], columns, width) for tap in range(3)]
            for part in range(2)
        ]

    def tile(lanes, width):
        w = weights(lanes, width)
        for r in range(row_count):
            late = [
                [
                    spatial(before_a, before_b, 1, r, part, lanes),
                    spatial(mine_a, mine_b, 0, r, part, lanes),
                    spatial(mine_a, mine_b, 1, r, part, lanes),
                ]
                for part in range(2)
            ]
            mixed = [w[p][0] * late[p][0] + w[p][1] * late[p][1] + w[p][2] * late[p][2] for p in range(2)]
            frame1[r, :, lanes] = gate(*mixed).astype(BF16)
            if not 1 <= r <= sent:
                mixed = [
                    w[p][0] * spatial(before_a, before_b, 0, r, p, lanes)
                    + w[p][1] * late[p][0]
                    + w[p][2] * late[p][1]
                    for p in range(2)
                ]
                frame0[r, :, lanes] = gate(*mixed).astype(BF16)

    lane_tiles(channels, tile)

    @pl.when(info[3] == 1)
    def _():
        def first_tile(lanes, width):
            w = weights(lanes, width)
            for r in range(1, sent + 1):
                mixed = [w[p][2] * mine_s0[r - 1, p, :, lanes].astype(F32) for p in range(2)]
                frame0[r, :, lanes] = gate(*mixed).astype(BF16)

        lane_tiles(channels, first_tile)

    copies = [
        pltpu.make_async_copy(frame0, out.at[0], sems.at[0]),
        pltpu.make_async_copy(frame1, out.at[1], sems.at[1]),
    ]
    for copy in copies:
        copy.start()
    for copy in copies:
        copy.wait()


def place_kernel(info, rows, gated, out, sem):
    @pl.when(info[3] == 0)
    def _():
        copy = pltpu.make_async_copy(rows, out.at[0, pl.ds(1, rows.shape[0])], sem)
        copy.start()
        copy.wait()


def head_mask(width):
    row = lax.broadcasted_iota(jnp.int32, (width, width), 0) // HEAD_DIM
    column = lax.broadcasted_iota(jnp.int32, (width, width), 1) // HEAD_DIM
    return row == column


def lane_groups(channels):
    return [(at, min(LANES, channels - at)) for at in range(0, channels, LANES)]


def state_kernel(key, value, state):
    tokens, channels = key.shape
    chunk = state.shape[2]
    ones = jnp.ones((8, tokens), BF16)
    state[...] = jnp.zeros_like(state)
    for at, width in lane_groups(channels):
        keys = jnp.maximum(key[:, at : at + width], 0)
        product = lax.dot_general(
            keys, value[:, at : at + width], (((0,), (0,)), ((), ())), preferred_element_type=F32
        )
        product = jnp.where(head_mask(width), product, 0.0)
        folded = sum(product[d : d + HEAD_DIM] for d in range(0, width, HEAD_DIM))
        lanes = slice(at % chunk, at % chunk + width)
        state[at // chunk, :HEAD_DIM, lanes] = folded
        state[at // chunk, HEAD_DIM:, lanes] = jnp.dot(ones, keys, preferred_element_type=F32)


def split(value):
    high = value.astype(BF16)
    return (high, (value - high.astype(F32)).astype(BF16))


def attend_kernel(query, state, out):
    channels = query.shape[1]
    chunk = state.shape[2]
    for at, width in lane_groups(channels):
        rows = jnp.maximum(query[:, at : at + width], 0)
        lanes = slice(at % chunk, at % chunk + width)
        mask = head_mask(width)
        folded = state[at // chunk, :HEAD_DIM, lanes]
        kv = jnp.where(mask, jnp.concatenate([folded] * (width // HEAD_DIM), axis=0), 0.0)
        sums = jnp.where(
            mask, jnp.broadcast_to(state[at // chunk, HEAD_DIM : HEAD_DIM + 1, lanes], (width, width)), 0.0
        )
        numerator = sum(jnp.dot(rows, part, preferred_element_type=F32) for part in split(kv))
        denominator = sum(
            lax.dot_general(rows, part, (((1,), (1,)), ((), ())), preferred_element_type=F32)
            for part in split(sums)
        )
        out[:, at : at + width] = (numerator / (denominator + 1.0)).astype(BF16)


def local_state(key, value, chunks):
    channels = key.shape[1]
    groups = pl.cdiv(pl.cdiv(channels, LANES), chunks)
    return kernel_call(state_kernel, jax.ShapeDtypeStruct((chunks, STATE_ROWS, groups * LANES), F32), (key, value))


def attend(query, state):
    return kernel_call(attend_kernel, jax.ShapeDtypeStruct(query.shape, BF16), (query, state))


def layer(query_proj, key_proj, value_proj, expanded, spatial_weight, temporal_weight):
    frames, row_count, col_count, channels = query_proj.shape
    hidden = expanded.shape[4]
    assert frames == 2 and row_count >= 4
    sent = SENT_ROWS if row_count == 8 else row_count - 2
    space, spaces = (lax.axis_index("space"), lax.axis_size("space"))
    info = jnp.stack(
        [space > 0, space < spaces - 1, space, lax.axis_index("tm") == 0]
    ).astype(jnp.int32)

    def tokens(array):
        return array.reshape(-1, channels)

    held = lax.optimization_barrier(jnp.transpose(expanded, (0, 1, 3, 2, 4)))
    after = shifted(held[0, : sent + 2], "tm", -1)

    mine_a = interior(
        held, spatial_weight, ((1, tuple(range(1, row_count - 1))), (0, tuple(range(sent + 1, row_count - 1))))
    )
    before_a = shifted(mine_a, "tm", 1)

    state = local_state(tokens(key_proj), tokens(value_proj), spaces)
    chunk = state.shape[2]
    slabs = slab_places(chunk, hidden)[-1][0] + 1
    packs, first_of, top_at, bottom_at = ([], [], None, None)
    for step in range(1, spaces):
        edges = "either" if spaces == 2 else {1: "tail", spaces - 1: "head"}.get(step)
        edge_rows = 4 if edges else 0
        if edges in ("tail", "either"):
            top_at = step - 1
        if edges in ("head", "either"):
            bottom_at = step - 1
        packed = kernel_call(
            functools.partial(pack_kernel, edges),
            jax.ShapeDtypeStruct((edge_rows + slabs, col_count, hidden), BF16),
            (jnp.stack([(space + step) % spaces, space]).astype(jnp.int32), held, state),
            [SMEM, VMEM, VMEM],
        )
        packs.append(rotated(packed, "space", step))
        first_of.append(edge_rows)

    mine_s0 = interior(held, spatial_weight, ((0, tuple(range(1, sent + 1))),))
    mine_b, own = kernel_call(
        functools.partial(boundary_kernel, len(packs), tuple(first_of), top_at, bottom_at),
        (
            jax.ShapeDtypeStruct((4, 2, col_count, hidden), BF16),
            jax.ShapeDtypeStruct((STATE_ROWS, chunk), F32),
        ),
        (info, held, spatial_weight, state, *packs),
        [SMEM] + [VMEM] * (3 + len(packs)),
    )
    step = 1
    while step < lax.axis_size("tm"):
        own = own + shifted(own.astype(BF16), "tm", step).astype(F32)
        step *= 2
    before_b = shifted(mine_b, "tm", 1)

    theirs = kernel_call(
        theirs_kernel,
        jax.ShapeDtypeStruct((sent, col_count, hidden), BF16),
        (after, mine_s0, mine_a, spatial_weight, temporal_weight),
    )
    returned = shifted(theirs, "tm", 1)

    whole = lax.dynamic_update_index_in_dim(state, own, space, 0)
    for step in range(1, spaces):
        whole = lax.dynamic_update_index_in_dim(whole, rotated(own, "space", step), (space - step) % spaces, 0)
    attended = attend(tokens(query_proj), whole).reshape(query_proj.shape)

    gated_shape = jax.ShapeDtypeStruct((2, row_count, col_count, hidden), BF16)
    gated = kernel_call(
        functools.partial(ours_kernel, sent),
        gated_shape,
        (info, mine_a, mine_b, mine_s0, before_a, before_b, temporal_weight),
        [SMEM] + [VMEM] * 6,
        ANY,
        [pltpu.VMEM(gated_shape.shape[1:], BF16)] * 2 + [pltpu.SemaphoreType.DMA((2,))],
    )
    gated = kernel_call(
        place_kernel, gated_shape, (info, returned, gated), [SMEM, VMEM, ANY], ANY, [pltpu.SemaphoreType.DMA], {2: 0}
    )
    return (attended, gated)


def solution(mesh):
    return jax.shard_map(
        layer,
        mesh=mesh,
        in_specs=(
            P(("groups", "tm"), "space", None, "mp"),
            P(("groups", "tm"), "space", None, "mp"),
            P(("groups", "tm"), "space", None, "mp"),
            P(("groups", "tm"), "space", None, None, "mp"),
            P(None, None, None, "mp"),
            P(None, None, "mp"),
        ),
        out_specs=(
            P(("groups", "tm"), "space", None, "mp"),
            P(("groups", "tm"), "space", None, "mp"),
        ),
        check_vma=False,
    )
```

```python
import functools

import jax
import jax.numpy as jnp
from jax import lax
from jax.experimental import pallas as pl
from jax.experimental.pallas import tpu as pltpu
from jax.sharding import PartitionSpec as P


HEAD_DIM = 32
LANES = 128
STATE_ROWS = HEAD_DIM + 8
BLOCK = 8
TOP, BOTTOM, SPACE, SPAN, EVEN = range(5)
F32 = jnp.float32
BF16 = jnp.bfloat16


def counter_ring(value, upward):
    groups, count = (lax.axis_size("groups"), lax.axis_size("tm"))
    pairs = []
    for group in range(groups):
        other = group ^ 1
        ahead = 1 if (group % 2 == 0) == upward else -1
        for at in range(count):
            target = (group, at + ahead)
            if not 0 <= at + ahead < count:
                target = (other, at) if other < groups else (group, (at + ahead) % count)
            pairs.append((group * count + at, target[0] * count + target[1]))
    return lax.ppermute(value, ("groups", "tm"), pairs)


def rotated(value, axis, steps):
    count = lax.axis_size(axis)
    return lax.ppermute(value, axis, [(source, (source + steps) % count) for source in range(count)])


VMEM = pl.BlockSpec(memory_space=pltpu.VMEM)
SMEM = pl.BlockSpec(memory_space=pltpu.SMEM)
ANY = pl.BlockSpec(memory_space=pl.ANY)


def kernel_call(kernel, out_shape, operands, specs=None, out_specs=None, scratch=(), aliases=None, vmem_mib=16):
    many = isinstance(out_shape, tuple)
    return pl.pallas_call(
        kernel,
        out_shape=out_shape,
        in_specs=[VMEM] * len(operands) if specs is None else specs,
        out_specs=out_specs if out_specs is not None else ((VMEM,) * len(out_shape) if many else VMEM),
        scratch_shapes=scratch,
        input_output_aliases=aliases or {},
        compiler_params=pltpu.CompilerParams(vmem_limit_bytes=vmem_mib << 20),
    )(*operands)


def lane_tiles(channels, body):
    full = channels // LANES

    @pl.loop(0, full)
    def _(tile):
        body(pl.ds(pl.multiple_of(tile * LANES, LANES), LANES), LANES)

    if channels % LANES:
        body(pl.ds(full * LANES, channels % LANES), channels % LANES)


def spread(row, columns, width):
    return jnp.broadcast_to(row, (columns, width))


def tap_weights(weight_ref, part, lanes, width, columns):
    column = lax.broadcasted_iota(jnp.int32, (columns, width), 0)
    taps = []
    for row_tap in range(3):
        row = []
        for col_tap in range(3):
            w = spread(weight_ref[row_tap, col_tap, part : part + 1, lanes], columns, width)
            if col_tap == 0:
                w = jnp.where(column == columns - 1, 0.0, w)
            if col_tap == 2:
                w = jnp.where(column == 0, 0.0, w)
            row.append(w)
        taps.append(row)
    return taps


def conv_row(above, here, below, taps, columns):
    sums = [taps[0][b] * above + taps[1][b] * here + taps[2][b] * below for b in range(3)]
    total = sums[1] + pltpu.roll(sums[0], 1, 0) + pltpu.roll(sums[2], columns - 1, 0)
    return total.astype(BF16)


def conv_interior(load, wanted, taps, columns):
    held = {}

    def row(r):
        if r not in held:
            held[r] = load(r)
        return held[r]

    return [conv_row(row(r - 1), row(r), row(r + 1), taps, columns) for r in wanted]


def either(flag, body, first, second):
    @pl.when(flag)
    def _():
        body(first, second)

    @pl.when(jnp.logical_not(flag))
    def _():
        body(second, first)


def conv_a_kernel(info, frames, weight, first, second):
    columns, channels = frames.shape[3:]
    count = first.shape[0]

    def body(out, raw):
        def tile(lanes, width):
            for part in range(2):
                taps = tap_weights(weight, part, lanes, width, columns)
                for r in range(count):
                    raw[r, part, :, lanes] = frames[0, r, part, :, lanes]

                def load(r, part=part):
                    return frames[1, r, part, :, lanes].astype(F32)

                for at, value in enumerate(conv_interior(load, range(1, count + 1), taps, columns)):
                    out[at, part, :, lanes] = value

        lane_tiles(channels, tile)

    either(info[EVEN] == 1, body, first, second)


def conv_s0_kernel(wanted, frames, weight, out):
    columns, channels = frames.shape[3:]

    def tile(lanes, width):
        for part in range(2):
            taps = tap_weights(weight, part, lanes, width, columns)

            def load(r, part=part):
                return frames[0, r, part, :, lanes].astype(F32)

            for at, value in enumerate(conv_interior(load, wanted, taps, columns)):
                out[at, part, :, lanes] = value

    lane_tiles(channels, tile)


def slab_places(chunk, channels):
    per_slab = channels // chunk
    return [(block // per_slab, block % per_slab * chunk) for block in range(STATE_ROWS // BLOCK)]


def pack_kernel(edges, step, info, frames, state, out):
    row_count, _, columns, channels = frames.shape[1:]
    chunks, _, chunk = state.shape
    index = lax.rem(info[SPACE] + step, chunks)
    at = 0
    if edges is not None:
        row = {
            "either": jnp.where(info[SPACE] == 0, row_count - 1, 0),
            "head": 0,
            "tail": row_count - 1,
        }[edges]
        for frame in range(2):
            for part in range(2):
                out[at] = frames[frame, row, part]
                at += 1
    places = slab_places(chunk, channels)
    for slab in range(places[-1][0] + 1):
        out[at + slab] = jnp.zeros((columns, channels), BF16)
    for block, (slab, lane) in enumerate(places):
        out[at + slab, :, lane : lane + chunk] = state[
            index, block * BLOCK : (block + 1) * BLOCK, :
        ].astype(BF16)


def boundary_kernel(n_packs, first_of, top_at, bottom_at, info, frames, weight, state, *refs):
    packs, (out, first, second, total, rounded) = (refs[:n_packs], refs[n_packs:])
    row_count, _, columns, channels = frames.shape[1:]
    has_top, has_bottom = (info[TOP].astype(F32), info[BOTTOM].astype(F32))
    chunk = state.shape[2]
    joined = first.shape[0] - 2

    def body(spatial, raw):
        def tile(lanes, width):
            for part in range(2):
                taps = tap_weights(weight, part, lanes, width, columns)
                for i in range(2):
                    raw[i, part, :, lanes] = frames[0, row_count - 2 + i, part, :, lanes]
                for i in range(joined):
                    raw[2 + i, part, :, lanes] = jnp.zeros((columns, width), BF16)
                for frame in range(2):

                    def load(r, frame=frame, part=part):
                        if r < 0:
                            return packs[top_at][2 * frame + part, :, lanes].astype(F32) * has_top
                        if r == row_count:
                            return packs[bottom_at][2 * frame + part, :, lanes].astype(F32) * has_bottom
                        return frames[frame, r, part, :, lanes].astype(F32)

                    values = conv_interior(load, (0, row_count - 1), taps, columns)
                    for i, value in enumerate(values):
                        out[2 * frame + i, part, :, lanes] = value
                        if frame == 1:
                            spatial[i, part, :, lanes] = value
                    if frame == 0 and joined == 2:
                        for i, value in enumerate(values):
                            spatial[2 + i, part, :, lanes] = value

        lane_tiles(channels, tile)
        if joined == 1:
            spatial[2] = out[jnp.where(info[SPACE] == 0, 1, 0)]

    either(info[EVEN] == 1, body, first, second)
    for block, (slab, lane) in enumerate(slab_places(chunk, channels)):
        rows = slice(block * BLOCK, (block + 1) * BLOCK)
        value = state[info[SPACE], rows, :]
        for pack, begin in zip(packs, first_of):
            value = value + pack[begin + slab, :, lane : lane + chunk].astype(F32)
        total[rows, :] = value
        rounded[rows, :] = value.astype(BF16)


def scan_kernel(step, info, own, earlier, total, rounded):
    value = own[...] + jnp.where(info[SPAN] >= step, earlier[...].astype(F32), 0.0)
    total[...] = value
    rounded[...] = value.astype(BF16)


def gate(value, key):
    return value * (key / (1.0 + jnp.exp(-key)))


def theirs_kernel(wanted, edge, info, first, second, *refs):
    if edge is None:
        sent_first, sent_second, s0, weight, temporal, out = refs
    else:
        last_first, last_second, sent_first, sent_second, b, s0, weight, temporal, out = refs
    columns, channels = first.shape[2:]
    held_rows = first.shape[0]
    row_count = held_rows + 2

    def body(ahead, behind):
        raw, s1 = (behind[0], ahead[1])

        def tile(lanes, width):
            mixed = []
            for part in range(2):
                taps = tap_weights(weight, part, lanes, width, columns)
                w = [spread(temporal[tap, part : part + 1, lanes], columns, width) for tap in range(3)]
                held = {}

                def load(r, part=part, held=held):
                    if r not in held:
                        ref, at = (raw, r) if r < held_rows else (behind[2], r - held_rows)
                        held[r] = ref[at, part, :, lanes].astype(F32)
                    return held[r]

                values = conv_interior(load, wanted, taps, columns)
                rows = [
                    w[0] * s0[r - 1, part, :, lanes].astype(F32)
                    + w[1] * s1[r - 1, part, :, lanes].astype(F32)
                    + w[2] * value.astype(F32)
                    for r, value in zip(wanted, values)
                ]
                if edge:
                    at_start = info[SPACE] == 0
                    last = row_count - 1
                    value = conv_row(
                        jnp.where(at_start, 0.0, load(last - 1)),
                        jnp.where(at_start, load(0), load(last)),
                        jnp.where(at_start, load(1), 0.0),
                        taps,
                        columns,
                    )
                    at = jnp.where(at_start, 0, 1)
                    rows.append(
                        w[0] * b[at, part, :, lanes].astype(F32)
                        + w[1] * b[2 + at, part, :, lanes].astype(F32)
                        + w[2] * value.astype(F32)
                    )
                mixed.append(rows)
            for r in range(out.shape[0]):
                out[r, :, lanes] = gate(mixed[0][r], mixed[1][r]).astype(BF16)

        lane_tiles(channels, tile)

    pair = ((first, sent_first), (second, sent_second))
    if edge is not None:
        pair = (pair[0] + (last_first,), pair[1] + (last_second,))
    either(info[EVEN] == 1, body, *pair)


def ours_kernel(
    joined, info, first, second, b_first, b_second, sent_first, sent_second, mine_b, mine_s0, temporal, out, late, early, sems
):
    row_count, columns, channels = late.shape
    alive = jnp.where(info[SPAN] == 0, 0.0, 1.0)
    at_start = info[SPACE] == 0

    def weights(lanes, width):
        return [
            [spread(temporal[tap, part : part + 1, lanes], columns, width) for tap in range(3)]
            for part in range(2)
        ]

    def late_copy():
        return pltpu.make_async_copy(late, out.at[1], sems.at[0])

    def early_copy(at, row):
        return pltpu.make_async_copy(early.at[at], out.at[0, row], sems.at[1 + at])

    def body(ahead, behind):
        before_a, before_b, mine_a = (ahead[0], ahead[1], behind[2])

        def load(ref, at, part, lanes):
            return ref[at, part, :, lanes].astype(F32)

        def last_frame(lanes, width):
            w = weights(lanes, width)
            for r in range(row_count):
                edge, end = (r in (0, row_count - 1), int(r > 0))
                mixed = []
                for p in range(2):
                    before = load(before_b, end, p, lanes) if edge else load(before_a, r - 1, p, lanes)
                    s0 = load(mine_b, end, p, lanes) if edge else load(mine_s0, r - 1, p, lanes)
                    s1 = load(mine_b, 2 + end, p, lanes) if edge else load(mine_a, r - 1, p, lanes)
                    mixed.append((w[p][0] * alive) * before + w[p][1] * s0 + w[p][2] * s1)
                late[r, :, lanes] = gate(*mixed).astype(BF16)

        def joined_rows(lanes, width):
            w = weights(lanes, width)
            for i in range(joined):
                end = jnp.where(at_start, 1, 0) if joined == 1 else i
                mixed = [
                    (w[p][0] * alive) * load(before_b, 2 + i, p, lanes)
                    + (w[p][1] * alive) * load(before_b, end, p, lanes)
                    + w[p][2] * load(mine_b, end, p, lanes)
                    for p in range(2)
                ]
                early[i, :, lanes] = gate(*mixed).astype(BF16)

        lane_tiles(channels, last_frame)
        late_copy().start()
        lane_tiles(channels, joined_rows)

    either(
        info[EVEN] == 1,
        body,
        (first, b_first, sent_second),
        (second, b_second, sent_first),
    )
    if joined == 1:
        ends = [jnp.where(at_start, row_count - 1, 0)]
    else:
        ends = [0, row_count - 1]
    for i, row in enumerate(ends):
        early_copy(i, row).start()

    @pl.when(info[SPAN] == 0)
    def _():
        def made(lanes, width):
            w = weights(lanes, width)
            for r in range(row_count - 2):
                mixed = [w[p][2] * mine_s0[r, p, :, lanes].astype(F32) for p in range(2)]
                early[joined + r, :, lanes] = gate(*mixed).astype(BF16)
            if joined == 1:
                mixed = [w[p][2] * mine_b[jnp.where(at_start, 0, 1), p, :, lanes].astype(F32) for p in range(2)]
                early[joined + row_count - 2, :, lanes] = gate(*mixed).astype(BF16)

        lane_tiles(channels, made)
        rows = list(range(1, row_count - 1))
        if joined == 1:
            rows.append(jnp.where(at_start, 0, row_count - 1))
        for r, row in enumerate(rows):
            early_copy(joined + r, row).start()
        for r, row in enumerate(rows):
            early_copy(joined + r, row).wait()

    for i, row in enumerate(ends):
        early_copy(i, row).wait()
    late_copy().wait()


def place_kernel(joined, row_count, info, rows, more, gated, out, sems):
    @pl.when(info[SPAN] != 0)
    def _():
        copies = []
        for r in range(row_count - 2 + 2 - joined):
            source = rows.at[r] if r < rows.shape[0] else more.at[r - rows.shape[0]]
            target = r + 1 if r < row_count - 2 else jnp.where(info[SPACE] == 0, 0, row_count - 1)
            copies.append(pltpu.make_async_copy(source, out.at[0, target], sems.at[r]))
        for copy in copies:
            copy.start()
        for copy in copies:
            copy.wait()


def head_mask(width):
    row = lax.broadcasted_iota(jnp.int32, (width, width), 0) // HEAD_DIM
    column = lax.broadcasted_iota(jnp.int32, (width, width), 1) // HEAD_DIM
    return row == column


def lane_groups(channels):
    return [(at, min(LANES, channels - at)) for at in range(0, channels, LANES)]


def state_kernel(key, value, state):
    tokens, channels = key.shape
    chunk = state.shape[2]
    ones = jnp.ones((8, tokens), BF16)
    state[...] = jnp.zeros_like(state)
    for at, width in lane_groups(channels):
        keys = jnp.maximum(key[:, at : at + width], 0)
        product = lax.dot_general(
            keys, value[:, at : at + width], (((0,), (0,)), ((), ())), preferred_element_type=F32
        )
        product = jnp.where(head_mask(width), product, 0.0)
        folded = sum(product[d : d + HEAD_DIM] for d in range(0, width, HEAD_DIM))
        lanes = slice(at % chunk, at % chunk + width)
        state[at // chunk, :HEAD_DIM, lanes] = folded
        state[at // chunk, HEAD_DIM:, lanes] = jnp.dot(ones, keys, preferred_element_type=F32)


def split(value):
    high = value.astype(BF16)
    return (high, (value - high.astype(F32)).astype(BF16))


def attend_kernel(info, query, own, *refs):
    others, (out, held) = (refs[:-2], refs[-2:])
    channels = query.shape[1]
    chunks, _, chunk = held.shape
    held[info[SPACE]] = own[...]
    for step, other in enumerate(others):
        held[lax.rem(info[SPACE] + (chunks - 1 - step), chunks)] = other[...]
    for at, width in lane_groups(channels):
        rows = jnp.maximum(query[:, at : at + width], 0)
        lanes = slice(at % chunk, at % chunk + width)
        mask = head_mask(width)
        folded = held[at // chunk, :HEAD_DIM, lanes]
        kv = jnp.where(mask, jnp.concatenate([folded] * (width // HEAD_DIM), axis=0), 0.0)
        sums = jnp.where(
            mask, jnp.broadcast_to(held[at // chunk, HEAD_DIM : HEAD_DIM + 1, lanes], (width, width)), 0.0
        )
        numerator = sum(jnp.dot(rows, part, preferred_element_type=F32) for part in split(kv))
        denominator = sum(
            lax.dot_general(rows, part, (((1,), (1,)), ((), ())), preferred_element_type=F32)
            for part in split(sums)
        )
        out[:, at : at + width] = (numerator / (denominator + 1.0)).astype(BF16)


def local_state(key, value, chunks):
    channels = key.shape[1]
    groups = pl.cdiv(pl.cdiv(channels, LANES), chunks)
    return kernel_call(state_kernel, jax.ShapeDtypeStruct((chunks, STATE_ROWS, groups * LANES), F32), (key, value))


def layer(query_proj, key_proj, value_proj, expanded, spatial_weight, temporal_weight):
    frames, row_count, col_count, channels = query_proj.shape
    hidden = expanded.shape[4]
    assert frames == 2 and row_count >= 6
    space, spaces = (lax.axis_index("space"), lax.axis_size("space"))
    joined = 1 if spaces == 2 else 2
    interior = row_count - 2
    early_rows = interior - 2
    info = jnp.stack(
        [space > 0, space < spaces - 1, space, lax.axis_index("tm"), lax.axis_index("groups") % 2 == 0]
    ).astype(jnp.int32)

    def tokens(array):
        return array.reshape(-1, channels)

    def rows_of(count):
        return jax.ShapeDtypeStruct((count, 2, col_count, hidden), BF16)

    held = lax.optimization_barrier(jnp.transpose(expanded, (0, 1, 3, 2, 4)))
    sent_first, sent_second = kernel_call(
        conv_a_kernel, (rows_of(interior), rows_of(interior)), (info, held, spatial_weight), [SMEM, VMEM, VMEM]
    )
    first = counter_ring(sent_first, True)
    second = counter_ring(sent_second, False)

    state = local_state(tokens(key_proj), tokens(value_proj), spaces)
    chunk = state.shape[2]
    slabs = slab_places(chunk, hidden)[-1][0] + 1
    packs, first_of, top_at, bottom_at = ([], [], None, None)
    for step in range(1, spaces):
        edges = "either" if spaces == 2 else {1: "tail", spaces - 1: "head"}.get(step)
        edge_rows = 4 if edges else 0
        if edges in ("tail", "either"):
            top_at = step - 1
        if edges in ("head", "either"):
            bottom_at = step - 1
        packed = kernel_call(
            functools.partial(pack_kernel, edges, step),
            jax.ShapeDtypeStruct((edge_rows + slabs, col_count, hidden), BF16),
            (info, held, state),
            [SMEM, VMEM, VMEM],
        )
        packs.append(rotated(packed, "space", step))
        first_of.append(edge_rows)

    mine_s0 = kernel_call(
        functools.partial(conv_s0_kernel, tuple(range(1, row_count - 1))), rows_of(interior), (held, spatial_weight)
    )
    summed = (jax.ShapeDtypeStruct((STATE_ROWS, chunk), F32), jax.ShapeDtypeStruct((STATE_ROWS, chunk), BF16))
    mine_b, b_sent_first, b_sent_second, own, rounded = kernel_call(
        functools.partial(boundary_kernel, len(packs), tuple(first_of), top_at, bottom_at),
        (rows_of(4), rows_of(2 + joined), rows_of(2 + joined)) + summed,
        (info, held, spatial_weight, state, *packs),
        [SMEM] + [VMEM] * (3 + len(packs)),
    )
    step = 1
    while step < lax.axis_size("tm"):
        earlier = rotated(rounded, "tm", step)
        own, rounded = kernel_call(
            functools.partial(scan_kernel, step), summed, (info, own, earlier), [SMEM, VMEM, VMEM]
        )
        step *= 2
    b_first = counter_ring(b_sent_first, True)
    b_second = counter_ring(b_sent_second, False)

    theirs_early = kernel_call(
        functools.partial(theirs_kernel, tuple(range(1, early_rows + 1)), None),
        jax.ShapeDtypeStruct((early_rows, col_count, hidden), BF16),
        (info, first, second, sent_first, sent_second, mine_s0, spatial_weight, temporal_weight),
        [SMEM] + [VMEM] * 7,
    )
    back_early = rotated(theirs_early, "tm", 1)
    late_rows = tuple(range(early_rows + 1, interior + 1))
    theirs_late = kernel_call(
        functools.partial(theirs_kernel, late_rows, joined == 1),
        jax.ShapeDtypeStruct((len(late_rows) + 2 - joined, col_count, hidden), BF16),
        (
            info, first, second, b_first, b_second, sent_first, sent_second, mine_b, mine_s0,
            spatial_weight, temporal_weight,
        ),
        [SMEM] + [VMEM] * 10,
    )
    back_late = rotated(theirs_late, "tm", 1)

    others = [rotated(own, "space", step) for step in range(1, spaces)]
    attended = kernel_call(
        attend_kernel,
        jax.ShapeDtypeStruct((query_proj.size // channels, channels), BF16),
        (info, tokens(query_proj), own, *others),
        [SMEM] + [VMEM] * (2 + len(others)),
        scratch=[pltpu.VMEM((spaces, STATE_ROWS, chunk), F32)],
    ).reshape(query_proj.shape)

    gated_shape = jax.ShapeDtypeStruct((2, row_count, col_count, hidden), BF16)
    gated = kernel_call(
        functools.partial(ours_kernel, joined),
        gated_shape,
        (info, first, second, b_first, b_second, sent_first, sent_second, mine_b, mine_s0, temporal_weight),
        [SMEM] + [VMEM] * 9,
        ANY,
        [
            pltpu.VMEM(gated_shape.shape[1:], BF16),
            pltpu.VMEM(gated_shape.shape[1:], BF16),
            pltpu.SemaphoreType.DMA((1 + row_count,)),
        ],
    )
    gated = kernel_call(
        functools.partial(place_kernel, joined, row_count),
        gated_shape,
        (info, back_early, back_late, gated),
        [SMEM, VMEM, VMEM, ANY],
        ANY,
        [pltpu.SemaphoreType.DMA((row_count,))],
        {3: 0},
    )
    return (attended, gated)


def solution(mesh):
    return jax.shard_map(
        layer,
        mesh=mesh,
        in_specs=(
            P(("groups", "tm"), "space", None, "mp"),
            P(("groups", "tm"), "space", None, "mp"),
            P(("groups", "tm"), "space", None, "mp"),
            P(("groups", "tm"), "space", None, None, "mp"),
            P(None, None, None, "mp"),
            P(None, None, "mp"),
        ),
        out_specs=(
            P(("groups", "tm"), "space", None, "mp"),
            P(("groups", "tm"), "space", None, "mp"),
        ),
        check_vma=False,
    )
```
